32 devices in a mesh: tm: 4 (over z), height: 8 (over y, x, core).
Axes of the slice: x: 2, y: 2, z: 4, core: 2. Of those that a mesh axis runs over, the one named last changes fastest.
Arguments:
- queries: bfloat16 [16, 16, 16, 2560], P('tm', 'height'), may hold values from -64 to 64
- keys: bfloat16 [16, 16, 16, 2560], P('tm', 'height'), may hold values from -64 to 64
- values: bfloat16 [16, 16, 16, 2560], P('tm', 'height'), may hold values from -6 to 6
- tile_mask: int32 [4, 8, 2, 18], P('tm', 'height'), may hold values 0 or 1
- sink_frame: int32 [1], replicated, may hold values from 0 to 15
Outputs:
- attended: bfloat16 [16, 16, 16, 2560], P('tm', 'height')
The draws below stay inside these ranges and needn't reach their ends.
All inputs are finite; a program needn't handle non-finite values. No bound on the sum of `tile_mask` on one device may be relied on, other than what follows from the above.
Results may differ from the reference program's by a relative error of at most 0.0041.
Values may be sent and summed in bfloat16 or wider, within the bound.
No kernel may reach another device: no remote copies, remote signals or barrier semaphores. Data moves between devices by JAX's collectives and lax.ppermute only.
A program may use at most 128 MiB of HBM per device.

```python
import math
import jax
import jax.numpy as jnp
from jax import lax

H = 20
HD = 128
TF = 4
TR = 2
TC = 8
COLS = 16
NEIGHBOURS = 18
FRAMES = 16
BANDS = 8
ROWS = 16
E = 2560
TT = 4
TW = 2


def shared_fields(key):
    shape = (FRAMES * ROWS * COLS, H * HD)
    key_field = jnp.clip(jax.random.normal(jax.random.fold_in(key, 21), shape, jnp.float32), -4.0, 4.0)
    query_field = jnp.clip(jax.random.normal(jax.random.fold_in(key, 22), shape, jnp.float32), -4.0, 4.0)
    final_shape = (FRAMES, ROWS, COLS, H * HD)
    return (query_field.reshape(final_shape), key_field.reshape(final_shape))


def draw_queries(key, part):
    return shared_fields(key)[0].astype(jnp.bfloat16)


def draw_keys(key, part):
    return shared_fields(key)[1].astype(jnp.bfloat16)


def with_ends(entries, rng, least, high):
    extent = entries.shape
    index_at = [jax.random.randint(jax.random.fold_in(rng, axis), (), 0, extent[axis]) for axis in range(len(extent))]
    entries = entries.at[tuple(index_at)].set(least)
    longest = extent.index(max(extent))
    index_at[longest] = (index_at[longest] + 1) % extent[longest]
    return entries.at[tuple(index_at)].set(high)


def shard_levels(stream_key, dims, cuts, low, high):
    def one(dim, shards_of):
        draws = jax.random.uniform(jax.random.fold_in(jax.random.fold_in(stream_key, 6), dim), (shards_of,), jnp.float32, low / len(cuts), high / len(cuts))
        return jnp.repeat(jnp.exp(draws), dims[dim] // shards_of).reshape((-1,) + (1,) * (len(dims) - dim - 1))

    factor_of = one(*cuts[0])
    for cut in cuts[1:]:
        factor_of = factor_of * one(*cut)
    return factor_of


def scatter_about(key, dims, width, bound, split=(), kind=jnp.bfloat16):
    drawn = jax.random.normal(key, dims, jnp.float32) * width
    if len(split) > 0:
        drawn = shard_levels(key, dims, split, -0.22, 0.18) * drawn
    return jnp.clip(drawn, min=-bound, max=bound).astype(kind)


def setup_inputs(seed: int = 0) -> dict:
    key_of = jax.random.split(jax.random.key(seed), 6)
    queries = draw_queries(jax.random.fold_in(key_of[5], 71), 0)
    keys = draw_keys(jax.random.fold_in(key_of[5], 71), 0)
    values = scatter_about(key_of[2], (FRAMES, ROWS, COLS, E), 1.0, 6.0, ((0, 4), (1, 8)))
    tile_mask = with_ends((jax.random.randint(key_of[3], (TT, BANDS, TW, NEIGHBOURS), 0, 4) < 3).astype(jnp.int32), jax.random.fold_in(key_of[3], 1), 0, 1)
    sink_frame = jax.random.randint(key_of[4], (1,), 0, FRAMES).astype(jnp.int32)
    return dict(queries=queries, keys=keys, values=values, tile_mask=tile_mask, sink_frame=sink_frame)


masked_score = -1e+30

def tile_allowed(tile_flags, time_base, band_index, band_total):
    q_tiles = tile_flags.shape[0]
    w_tiles = tile_flags.shape[1]
    q_time = jnp.arange(q_tiles)[:, None, None, None, None]
    q_width = jnp.arange(w_tiles)[None, :, None, None, None]
    k_time = jnp.arange(q_tiles + 1)[None, None, :, None, None]
    k_band = jnp.arange(3)[None, None, None, :, None] - 1
    k_width = jnp.arange(w_tiles)[None, None, None, None, :]
    time_step = k_time - 1 - q_time
    width_step = k_width - q_width
    nearby = (time_step >= -1) & (time_step <= 0) & (jnp.abs(width_step) <= 1)
    code_all = (time_step + 1) * 9 + (k_band + 1) * 3 + width_step + 1
    matches = code_all[..., None] == jnp.arange(tile_flags.shape[2])
    picked = lax.optimization_barrier(jnp.sum(jnp.where(matches, tile_flags[:, :, None, None, None, :], 0), axis=-1)) > 0
    itself = (time_step == 0) & (k_band == 0) & (width_step == 0)
    time_valid = time_base + k_time - 1 >= 0
    band_now = band_index + k_band
    band_valid = (band_now >= 0) & (band_now < band_total)
    return nearby & (picked | itself) & time_valid & band_valid

def token_allowed(tiles_ok, row_count):
    q_tiles, w_tiles, k_tiles = (tiles_ok.shape[0], tiles_ok.shape[1], tiles_ok.shape[2])
    grid = tiles_ok[:, None, None, :, None, :, None, :, None, :, None]
    full = jnp.broadcast_to(grid, (q_tiles, TF, row_count, w_tiles, TC, k_tiles, TF, 3, row_count, w_tiles, TC))
    return full.reshape(q_tiles * TF * row_count * w_tiles * TC, k_tiles * TF * 3 * row_count * w_tiles * TC)

def reference(queries, keys, values, tile_mask, sink_frame):
    scaling = 1.0 / math.sqrt(HD)
    key_pad = jnp.pad(keys, ((TF, 0), (TR, TR), (0, 0), (0, 0)))
    val_pad = jnp.pad(values, ((TF, 0), (TR, TR), (0, 0), (0, 0)))
    sink_index = sink_frame[0].astype(jnp.int32)
    sink_keys = lax.dynamic_index_in_dim(keys, sink_index, 0, keepdims=False).reshape(BANDS, TR * COLS, H, HD).astype(jnp.float32)
    sink_vals = lax.dynamic_index_in_dim(values, sink_index, 0, keepdims=False).reshape(BANDS, TR * COLS, H, HD).astype(jnp.float32)
    zero_index = jnp.zeros((), jnp.int32)

    def one_tile(tile_index):
        time_tile = (tile_index // BANDS).astype(jnp.int32)
        band_index = (tile_index % BANDS).astype(jnp.int32)
        q_block = lax.dynamic_slice(queries, (time_tile * TF, band_index * TR, zero_index, zero_index), (TF, TR, COLS, E))
        q_block = q_block.reshape(TF * TR * COLS, H, HD).astype(jnp.float32)
        k_block = lax.dynamic_slice(key_pad, (time_tile * TF, band_index * TR, zero_index, zero_index), (2 * TF, 3 * TR, COLS, E))
        k_block = k_block.reshape(-1, H, HD).astype(jnp.float32)
        v_block = lax.dynamic_slice(val_pad, (time_tile * TF, band_index * TR, zero_index, zero_index), (2 * TF, 3 * TR, COLS, E))
        v_block = v_block.reshape(-1, H, HD).astype(jnp.float32)
        tile_flags = lax.dynamic_slice(tile_mask, (time_tile, band_index, zero_index, zero_index), (1, 1, TW, NEIGHBOURS))[:, 0]
        allowed = token_allowed(tile_allowed(tile_flags, time_tile, band_index, BANDS), TR)
        scores = jnp.einsum('qhd,khd->hqk', q_block, k_block) * scaling
        scores = jnp.where(allowed[None], scores, masked_score)
        row_max = lax.optimization_barrier(jnp.max(scores, axis=-1))
        weights = jnp.exp(scores - row_max[..., None]).astype(jnp.bfloat16).astype(jnp.float32)
        row_sum = lax.optimization_barrier(jnp.sum(weights, axis=-1))
        window_out = jnp.einsum('hqk,khd->hqd', weights, v_block)
        sink_scores = jnp.einsum('qhd,rkhd->hqrk', q_block, sink_keys) * scaling
        sink_max = lax.optimization_barrier(jnp.max(sink_scores, axis=-1))
        sink_weights = jnp.exp(sink_scores - sink_max[..., None]).astype(jnp.bfloat16).astype(jnp.float32)
        sink_sum = lax.optimization_barrier(jnp.sum(sink_weights, axis=-1))
        top_score = jnp.maximum(row_max, lax.optimization_barrier(jnp.max(sink_max, axis=-1)))
        window_factor = jnp.exp(row_max - top_score)
        sink_factor = jnp.exp(sink_max - top_score[..., None])
        sink_out = jnp.einsum('hqrk,rkhd->hqd', sink_weights * sink_factor[..., None], sink_vals)
        numerator = window_factor[..., None] * window_out + sink_out
        denominator = window_factor * row_sum + lax.optimization_barrier(jnp.sum(sink_factor * sink_sum, axis=-1))
        result = numerator / denominator[..., None]
        return jnp.transpose(result, (1, 0, 2)).reshape(TF, TR, COLS, E).astype(jnp.bfloat16)
    blocks = lax.map(one_tile, jnp.arange(TT * BANDS, dtype=jnp.int32))
    blocks = blocks.reshape(TT, BANDS, TF, TR, COLS, E)
    return jnp.transpose(blocks, (0, 2, 1, 3, 4, 5)).reshape(FRAMES, ROWS, COLS, E)
```

```python
import math

import jax
import jax.numpy as jnp
from jax import lax
from jax.experimental import pallas as pl
from jax.experimental.pallas import tpu as pltpu
from jax.sharding import PartitionSpec as P

HD = 128
TF = 4
TC = 8
CHUNKS = 2
NEG = -1e30
AUX = 128


def split3(x):
    hi = x.astype(jnp.bfloat16).astype(jnp.float32)
    mid = (x - hi).astype(jnp.bfloat16).astype(jnp.float32)
    return hi, mid, x - hi - mid


def window_kernel(
    heads, group, scale, qo, qf, ao, af, k0, v0, k1, v1, k2, v2,
    acc_o, stat_o, pay, bias,
):
    step = pl.program_id(0)
    tokens = qo.shape[0]
    lane = lax.broadcasted_iota(jnp.int32, (tokens, AUX), 1)

    @pl.when(step == 0)
    def _():
        second = (lax.broadcasted_iota(jnp.int32, (tokens, tokens), 1) // TC) % 2 == 1
        for n, aux in enumerate((ao, af)):
            flags = aux[...].astype(jnp.float32)
            for j in range(3):
                one = jnp.broadcast_to(flags[:, 2 * j : 2 * j + 1], second.shape)
                two = jnp.broadcast_to(flags[:, 2 * j + 1 : 2 * j + 2], second.shape)
                kept = jnp.where(second, two, one) > 0.5
                bias[pl.ds(n * tokens, tokens), pl.ds(j * tokens, tokens)] = jnp.where(
                    kept, 0.0, NEG
                )
        stat_o[...] = jnp.zeros_like(stat_o)
        pay[:, pl.ds(heads * HD, AUX)] = jnp.zeros((tokens, AUX), pay.dtype)

    mo = stat_o[:, :AUX]
    lo = stat_o[:, AUX:]
    sent = pay[:, pl.ds(heads * HD, AUX)].astype(jnp.float32)
    for g in range(group):
        at = slice(g * HD, (g + 1) * HD)
        head = step * group + g
        q = jnp.concatenate((qo[:, at], qf[:, at]), axis=0)
        k = jnp.concatenate((k0[:, at], k1[:, at], k2[:, at]), axis=0)
        v = jnp.concatenate((v0[:, at], v1[:, at], v2[:, at]), axis=0)
        v = jnp.concatenate((v, jnp.ones_like(v)), axis=1)
        s = lax.dot_general(
            q, k, (((1,), (1,)), ((), ())), preferred_element_type=jnp.float32
        )
        s = s * scale + bias[...]
        m = jnp.max(s, axis=1, keepdims=True)
        p = jnp.exp2(s - m).astype(jnp.bfloat16)
        o = jnp.dot(p, v, preferred_element_type=jnp.float32)
        acc_o[:, at] = o[:tokens, :HD]
        mo = jnp.where(lane == head, m[:tokens], mo)
        lo = jnp.where(lane == head, o[:tokens, HD:], lo)
        out_at = pl.multiple_of(head * HD, HD)
        pay[:, pl.ds(out_at, HD)] = o[tokens:, :HD].astype(pay.dtype)
        parts = split3(m[tokens:]) + split3(o[tokens:, HD:])
        for i, part in enumerate(parts):
            sent = jnp.where(lane == head + i * heads, part, sent)
    stat_o[:, :AUX] = mo
    stat_o[:, AUX:] = lo
    pay[:, pl.ds(heads * HD, AUX)] = sent.astype(pay.dtype)


def window_call(chunk, heads, group, scale, qo, qf, ao, af, bands):
    tokens = qo.shape[0]
    steps = heads // group
    wide = group * HD
    first = chunk * steps
    full = pl.BlockSpec((tokens, wide), lambda i: (0, first + i))
    part = pl.BlockSpec((tokens, wide), lambda i: (0, i))
    aux_f = pl.BlockSpec((tokens, AUX), lambda i: (0, af))
    aux_o = pl.BlockSpec((tokens, AUX), lambda i: (0, 0))
    specs, args = [full, full, aux_o, aux_f], [qo, qf, ao, qf]
    for k, v in bands:
        for x in (k, v):
            if x.ndim == 2:
                specs.append(full)
            args.append(x)
    k2, v2 = bands[-1]
    specs = [full, full, aux_o, aux_f, full, full, full, full, part, part]
    whole = lambda shape: pl.BlockSpec(shape, lambda i: (0, 0))
    pairs = 2 * tokens * 3 * tokens * heads
    return pl.pallas_call(
        lambda *refs: window_kernel(heads, group, scale, *refs),
        grid=(steps,),
        in_specs=specs,
        out_specs=(part, whole((tokens, 2 * AUX)), whole((tokens, heads * HD + AUX))),
        out_shape=(
            jax.ShapeDtypeStruct((tokens, heads * HD), jnp.float32),
            jax.ShapeDtypeStruct((tokens, 2 * AUX), jnp.float32),
            jax.ShapeDtypeStruct((tokens, heads * HD + AUX), jnp.bfloat16),
        ),
        scratch_shapes=[pltpu.VMEM((2 * tokens, 3 * tokens), jnp.float32)],
        cost_estimate=pl.CostEstimate(
            flops=6 * pairs * HD, bytes_accessed=10 * tokens * heads * HD * 2, transcendentals=pairs
        ),
        name="window",
    )(*args)


def pick(x, lane, at):
    return jnp.sum(jnp.where(lane == at, x, 0.0), axis=1, keepdims=True)


def mirrored(count):
    places = [0]
    while len(places) < count:
        half = count // (2 * len(places))
        places += [p + half for p in places]
    return places


def final_kernel(heads, group, scale, rows, n_sink, *refs):
    q, acc_o, stat_o, got, got_stat, first = refs[:6]
    keys = refs[6 : 6 + n_sink]
    vals = refs[6 + n_sink : 6 + 2 * n_sink]
    out = refs[-1]
    step = pl.program_id(0)
    tokens = q.shape[0]
    lane = lax.broadcasted_iota(jnp.int32, (tokens, AUX), 1)
    mo, lo = stat_o[:, :AUX], stat_o[:, AUX:]
    theirs = got_stat[...].astype(jnp.float32)
    prior = first[0] > 0
    for g in range(group):
        at = slice(g * HD, (g + 1) * HD)
        head = step * group + g
        k = jnp.concatenate([r[:, at] for r in keys], axis=0)
        order = mirrored(vals[0].shape[0] // rows)
        v = jnp.concatenate([r[p * rows : (p + 1) * rows, at] for r in vals for p in order], axis=0)
        v = jnp.concatenate((v, jnp.ones_like(v)), axis=1)
        s = scale * lax.dot_general(
            q[:, at], k, (((1,), (1,)), ((), ())), preferred_element_type=jnp.float32
        )
        ms = jnp.max(s, axis=1, keepdims=True)
        m1 = pick(mo, lane, head)
        l1 = pick(lo, lane, head)
        at3 = [pick(theirs, lane, head + i * heads) for i in range(6)]
        m2 = jnp.where(prior, at3[0] + at3[1] + at3[2], NEG)
        l2 = at3[3] + at3[4] + at3[5]
        top = jnp.maximum(jnp.maximum(m1, m2), ms)
        p = jnp.exp2(s - ms).astype(jnp.bfloat16)
        o = jnp.dot(p, v, preferred_element_type=jnp.float32)
        es, e1, e2 = jnp.exp2(ms - top), jnp.exp2(m1 - top), jnp.exp2(m2 - top)
        num = es * o[:, :HD] + e1 * acc_o[:, at] + e2 * got[:, at].astype(jnp.float32)
        den = es * o[:, HD:] + e1 * l1 + e2 * l2
        out[:, at] = (num / den).astype(out.dtype)


def final_call(chunk, heads, group, scale, rows, q, state, got, first, keys, vals, out):
    tokens, features = q.shape
    acc_o, stat_o = state
    steps = heads // group
    wide = group * HD
    base = chunk * steps
    full = lambda x: pl.BlockSpec((x.shape[0], wide), lambda i: (0, base + i))
    part = pl.BlockSpec((tokens, wide), lambda i: (0, i))
    specs = [
        full(q),
        part,
        pl.BlockSpec((tokens, 2 * AUX), lambda i: (0, 0)),
        part,
        pl.BlockSpec((tokens, AUX), lambda i: (0, heads * HD // AUX)),
        pl.BlockSpec(memory_space=pltpu.SMEM),
    ]
    args = [q, acc_o, stat_o, got, got, first, *keys, *vals]
    specs += [full(x) for x in (*keys, *vals)]
    aliases = {}
    if out is not None:
        aliases = {len(args): 0}
        args.append(out)
        specs.append(pl.BlockSpec(memory_space=pl.ANY))
    pairs = tokens * sum(x.shape[0] for x in keys) * heads
    return pl.pallas_call(
        lambda *refs: final_kernel(heads, group, scale, rows, len(keys), *refs),
        grid=(steps,),
        in_specs=specs,
        out_specs=full(q),
        out_shape=jax.ShapeDtypeStruct((tokens, features), q.dtype),
        input_output_aliases=aliases,
        cost_estimate=pl.CostEstimate(
            flops=6 * pairs * HD,
            bytes_accessed=8 * tokens * heads * HD * 2,
            transcendentals=pairs,
        ),
        name="final",
    )(*args)


def swap(x, axis, bit):
    count = lax.axis_size(axis)
    return lax.ppermute(x, axis, [(i, i ^ bit) for i in range(count)])


def tile_flags(mask, slot, band, bands, steps, tokens, col_count):
    width_tiles = mask.shape[0]
    rows = []
    cq = jnp.arange(width_tiles)[:, None, None]
    dh = jnp.stack(steps)[None, :, None]
    ck = jnp.arange(width_tiles)[None, None, :]
    code = slot * 9 + (dh + 1) * 3 + ck - cq + 1
    hit = code[..., None] == jnp.arange(mask.shape[1])
    kept = jnp.sum(jnp.where(hit, mask[:, None, None, :], 0), axis=-1) > 0
    if slot == 1:
        kept = kept | ((dh == 0) & (ck == cq))
    kept = kept & (band + dh >= 0) & (band + dh < bands) & (jnp.abs(ck - cq) <= 1)
    kept = kept.reshape(width_tiles, -1).astype(jnp.float32)
    kept = jnp.pad(kept, ((0, 0), (0, AUX - kept.shape[1])))
    tile_of = (jnp.arange(tokens) % col_count) // TC
    full = jnp.zeros((tokens, AUX), jnp.float32)
    for c in range(width_tiles):
        full = jnp.where((tile_of == c)[:, None], kept[c][None], full)
    return full.astype(jnp.bfloat16)


def shards(queries, keys, values, tile_mask, sink_frame):
    frames, row_count, col_count, features = queries.shape
    tokens = frames * row_count * col_count
    head_count = features // HD
    scale = math.log2(math.e) / math.sqrt(HD)
    times, bands = lax.axis_size("tm"), lax.axis_size("height")
    t, h = lax.axis_index("tm"), lax.axis_index("height")
    assert frames == TF and col_count == 2 * TC and head_count % CHUNKS == 0
    assert times & (times - 1) == 0 and bands & (bands - 1) == 0 and bands > 1
    heads = head_count // CHUNKS
    wide = heads * HD
    group = 5 if heads % 5 == 0 else 1

    q, k, v = (x.reshape(tokens, features) for x in (queries, keys, values))

    owner, local = sink_frame[0] // frames, sink_frame[0] % frames
    rows = row_count * col_count
    sk = lax.dynamic_slice_in_dim(k, local * rows, rows, 0)
    sv = lax.dynamic_slice_in_dim(v, local * rows, rows, 0)
    cand = jnp.concatenate((sk, sv), axis=0)
    bit = 1
    while bit < times:
        other = swap(cand, "tm", bit)
        have = (t ^ owner) // bit == 0
        cand = jnp.where(have, cand, other)
        bit *= 2
    sk, sv = cand[:rows], cand[rows:]
    bits = [1 << b for b in range(1, bands.bit_length() - 1)]
    for b in range(len(bits)):
        sk = jnp.concatenate((sk, swap(sk, "height", bits[b])), axis=0)
        sv = jnp.concatenate((sv, swap(sv, "height", bits[-1 - b])), axis=0)
    sink_k = (sk, swap(sk, "height", 1))
    sink_v = (sv, swap(sv, "height", 1))

    core = 1 - 2 * (h % 2)
    steps = (jnp.zeros_like(core), core, -core)
    mask = tile_mask[0, 0]
    flags_own = tile_flags(mask, 1, h, bands, steps, tokens, col_count)
    flags_sent = tile_flags(mask, 0, h, bands, steps, tokens, col_count)

    odd = [(i, i + 1) for i in range(1, bands - 1, 2)]
    odd += [(j, i) for i, j in odd]
    near = []
    for c in range(CHUNKS):
        at = slice(c * wide, (c + 1) * wide)
        both = jnp.concatenate((k[:, at], v[:, at]), axis=0)
        near.append(lax.ppermute(both, "height", odd))
    core_k, core_v = swap(k, "height", 1), swap(v, "height", 1)
    q_sent = jnp.concatenate((q, flags_sent), axis=1)
    q_later = lax.ppermute(q_sent, "tm", [(i + 1, i) for i in range(times - 1)])

    states, got = [], []
    for c in range(CHUNKS):
        k2, v2 = near[c][:tokens], near[c][tokens:]
        acc, stat, pay = window_call(
            c, heads, group, scale, q, q_later, flags_own, features // AUX,
            ((k, v), (core_k, core_v), (k2, v2)),
        )
        states.append((acc, stat))
        got.append(lax.ppermute(pay, "tm", [(i, i + 1) for i in range(times - 1)]))
    first = (t > 0).astype(jnp.int32).reshape(1)
    out = None
    for c in range(CHUNKS):
        out = final_call(c, heads, group, scale, rows, q, states[c], got[c], first, sink_k, sink_v, out)
    return out.reshape(queries.shape)


def solution(mesh):
    spec = P("tm", "height", None, None)
    return jax.shard_map(
        shards,
        mesh=mesh,
        in_specs=(spec, spec, spec, spec, P()),
        out_specs=spec,
        check_vma=False,
    )
```

```python
import math

import jax
import jax.numpy as jnp
from jax import lax
from jax.experimental import pallas as pl
from jax.experimental.pallas import tpu as pltpu
from jax.sharding import PartitionSpec as P


HD = 128
TF = 4
TC = 8
CHUNKS = 2
NEG = -1e30
AUX = 128
GRANT = 12 << 20


def split3(x):
    hi = x.astype(jnp.bfloat16).astype(jnp.float32)
    mid = (x - hi).astype(jnp.bfloat16).astype(jnp.float32)
    return hi, mid, x - hi - mid


def dot(x, y, contract):
    dims = (((contract,), (contract,)), ((), ()))
    return lax.dot_general(x, y, dims, preferred_element_type=jnp.float32)


VMEM = pltpu.MemorySpace.VMEM


def near_core(x):
    return pltpu.with_memory_space_constraint(x, VMEM)


def lanes(head):
    return pl.ds(pl.multiple_of(head * HD, HD), HD)


def attend_kernel(chunk, heads, group, scale, places, q_part, own, *refs):
    q, flags = refs[:2]
    n_bands = len(places)
    keys = refs[2 : 2 + n_bands]
    vals = refs[2 + n_bands : 2 + 2 * n_bands]
    acc, stat, bias = refs[2 + 2 * n_bands :]
    tokens = q.shape[0]
    pad = stat.shape[0] // 2

    second = (lax.broadcasted_iota(jnp.int32, (tokens, tokens), 0) // TC) % 2 == 1
    kept = jnp.where(flags[:, flags.shape[1] - AUX :].astype(jnp.float32).T > 0.5, 0.0, NEG)
    for j in range(n_bands):
        one = jnp.broadcast_to(kept[2 * j : 2 * j + 1], second.shape)
        two = jnp.broadcast_to(kept[2 * j + 1 : 2 * j + 2], second.shape)
        bias[j * tokens : (j + 1) * tokens] = jnp.where(second, two, one)
    stat[...] = jnp.zeros_like(stat)

    def step(i, _):
        for g in range(group):
            head = i * group + g
            there = lanes(chunk * heads + head)
            here = lanes(head)
            k = jnp.concatenate(
                [
                    r[row * tokens : (row + 1) * tokens, here if part else there]
                    for r, (row, _, part) in zip(keys, places)
                ],
                axis=0,
            )
            v = jnp.concatenate(
                [
                    r[row * tokens : (row + 1) * tokens, here if part else there]
                    for r, (_, row, part) in zip(vals, places)
                ],
                axis=0,
            )
            s = dot(k, q[:, here if q_part else there], 1) * scale + bias[...]
            m = jnp.max(s, axis=0, keepdims=True)
            p = jnp.exp2(s - m).astype(jnp.bfloat16)
            acc[here] = dot(v, p, 0).astype(acc.dtype)
            stat[pl.ds(head, 1)] = m
            stat[pl.ds(pad + head, 1)] = jnp.sum(p.astype(jnp.float32), axis=0, keepdims=True)
        return 0

    lax.fori_loop(0, heads // group, step, 0)
    if not own:
        parts = split3(stat[:pad]) + split3(stat[pad:])[:2]
        for i, part in enumerate(parts):
            acc[heads * HD + i * pad : heads * HD + (i + 1) * pad] = part.astype(acc.dtype)


def padded(heads):
    return -(-heads // 16) * 16


def attend(chunk, heads, group, scale, q, q_part, flags, bands, own):
    tokens, pad = q.shape[0], padded(heads)
    args = [q, flags] + [b[0] for b in bands] + [b[1] for b in bands]
    places = [b[2:] for b in bands]
    keys = len(bands) * tokens
    stat = (2 * pad, tokens)
    vmem = pl.BlockSpec(memory_space=VMEM)
    if own:
        out_shape = (pltpu.VMEM((heads * HD, tokens), jnp.float32), pltpu.VMEM(stat, jnp.float32))
        scratch = []
    else:
        out_shape = (pltpu.VMEM((heads * HD + 5 * pad, tokens), jnp.bfloat16),)
        scratch = [pltpu.VMEM(stat, jnp.float32)]
    pairs = tokens * keys * heads
    return pl.pallas_call(
        lambda *refs: attend_kernel(chunk, heads, group, scale, places, q_part, own, *refs),
        in_specs=[vmem] * len(args),
        out_specs=(vmem,) * len(out_shape),
        out_shape=out_shape,
        scratch_shapes=scratch + [pltpu.VMEM((keys, tokens), jnp.float32)],
        cost_estimate=pl.CostEstimate(
            flops=6 * pairs * HD, bytes_accessed=10 * tokens * heads * HD * 2, transcendentals=pairs
        ),
        compiler_params=pltpu.CompilerParams(vmem_limit_bytes=GRANT),
        name="attend",
    )(*[near_core(x) for x in args])


def merge_kernel(heads, group, scale, n_sink, *refs):
    q, pieces = refs[0], refs[1 : 1 + n_sink]
    accs, stats, outs = (refs[1 + n_sink + i * CHUNKS :][:CHUNKS] for i in range(3))
    stat = refs[-1]
    rows = pieces[0].shape[0] // 2
    pad = padded(heads)
    stat[...] = jnp.zeros_like(stat)
    for c in range(CHUNKS):

        def step(i, _):
            for g in range(group):
                head = i * group + g
                there, here = lanes(c * heads + head), lanes(head)
                m1, l1 = stats[c][pl.ds(head, 1)], stats[c][pl.ds(pad + head, 1)]
                k = jnp.concatenate([r[:rows, there] for r in pieces], axis=0)
                v = jnp.concatenate([r[rows:, there] for r in pieces], axis=0)
                s = dot(k, q[:, there], 1) * scale
                top = jnp.maximum(jnp.max(s, axis=0, keepdims=True), m1)
                p = jnp.exp2(s - top).astype(jnp.bfloat16)
                f = jnp.exp2(m1 - top)
                outs[c][here] = dot(v, p, 0) + accs[c][here] * f
                total = jnp.sum(p.astype(jnp.float32), axis=0, keepdims=True) + f * l1
                stat[pl.ds(2 * c * pad + head, 1)] = top
                stat[pl.ds((2 * c + 1) * pad + head, 1)] = total
            return 0

        lax.fori_loop(0, heads // group, step, 0)


def merge_call(heads, group, scale, q, pieces, states):
    tokens = q.shape[0]
    args = [q, *pieces, *[s[0] for s in states], *[s[1] for s in states]]
    vmem = pl.BlockSpec(memory_space=VMEM)
    pairs = tokens * sum(x.shape[0] for x in pieces) // 2 * heads * CHUNKS
    shapes = [pltpu.VMEM(s[0].shape, jnp.float32) for s in states]
    shapes.append(pltpu.VMEM((2 * CHUNKS * padded(heads), tokens), jnp.float32))
    return pl.pallas_call(
        lambda *refs: merge_kernel(heads, group, scale, len(pieces), *refs),
        in_specs=[vmem] * len(args),
        out_specs=[vmem] * len(shapes),
        out_shape=shapes,
        cost_estimate=pl.CostEstimate(
            flops=6 * pairs * HD, bytes_accessed=8 * tokens * heads * HD * 2, transcendentals=pairs
        ),
        compiler_params=pltpu.CompilerParams(vmem_limit_bytes=GRANT),
        name="merge",
    )(*[near_core(x) for x in args])


def final_kernel(heads, group, scale, n_sink, *refs):
    q, first, stat_o = refs[:3]
    accs, gots = refs[3 : 3 + CHUNKS], refs[3 + CHUNKS : 3 + 2 * CHUNKS]
    pieces = refs[3 + 2 * CHUNKS : 3 + 2 * CHUNKS + n_sink]
    rows = pieces[0].shape[0] // 2
    out, state, done, sems = refs[-4:]
    pad = padded(heads)
    wide = group * HD
    turns = heads // group

    def copy(turn):
        at = pl.ds(pl.multiple_of(turn * wide, HD), wide)
        return pltpu.make_async_copy(done.at[:, at], out.at[:, at], sems.at[turn])

    for c in range(CHUNKS):
        got = gots[c]
        part = [
            got[heads * HD + i * pad : heads * HD + (i + 1) * pad].astype(jnp.float32)
            for i in range(5)
        ]
        m1 = stat_o[2 * c * pad : (2 * c + 1) * pad]
        l1 = stat_o[(2 * c + 1) * pad : (2 * c + 2) * pad]
        m2 = jnp.where(first[0] > 0, part[0] + part[1] + part[2], NEG)
        l2 = part[3] + part[4]
        m12 = jnp.maximum(m1, m2)
        e1, e2 = jnp.exp2(m1 - m12), jnp.exp2(m2 - m12)
        for i, x in enumerate((m12, e1, e2, e1 * l1 + e2 * l2)):
            state[i * pad : (i + 1) * pad] = x

        def step(i, _):
            for g in range(group):
                head = i * group + g
                there, here = lanes(c * heads + head), lanes(head)
                m12, e1, e2, l12 = (state[pl.ds(n * pad + head, 1)] for n in range(4))
                k = jnp.concatenate([r[:rows, there] for r in pieces], axis=0)
                v = jnp.concatenate([r[rows:, there] for r in pieces], axis=0)
                s = dot(k, q[:, there], 1) * scale
                top = jnp.maximum(jnp.max(s, axis=0, keepdims=True), m12)
                p = jnp.exp2(s - top).astype(jnp.bfloat16)
                f = jnp.exp2(m12 - top)
                den = jnp.sum(p.astype(jnp.float32), axis=0, keepdims=True) + f * l12
                inv = 1.0 / den
                theirs = got[here].astype(jnp.float32)
                res = dot(v, p, 0) * inv + accs[c][here] * (f * e1 * inv) + theirs * (f * e2 * inv)
                done[:, there] = res.T.astype(done.dtype)
            copy(c * turns + i).start()
            return 0

        lax.fori_loop(0, turns, step, 0)

    def end(i, _):
        copy(i).wait()
        return 0

    lax.fori_loop(0, CHUNKS * turns, end, 0)


def final_call(heads, group, scale, q, accs, stat, gots, first, pieces):
    tokens, features = q.shape
    args = [q, first, stat, *accs, *gots, *pieces]
    vmem = pl.BlockSpec(memory_space=VMEM)
    specs = [vmem] * len(args)
    specs[1] = pl.BlockSpec(memory_space=pltpu.SMEM)
    args = [x if i == 1 else near_core(x) for i, x in enumerate(args)]
    pairs = tokens * sum(x.shape[0] for x in pieces) // 2 * heads * CHUNKS
    return pl.pallas_call(
        lambda *refs: final_kernel(heads, group, scale, len(pieces), *refs),
        in_specs=specs,
        out_specs=pl.BlockSpec(memory_space=pltpu.MemorySpace.HBM),
        out_shape=jax.ShapeDtypeStruct((tokens, features), q.dtype),
        scratch_shapes=[
            pltpu.VMEM((4 * padded(heads), tokens), jnp.float32),
            pltpu.VMEM((tokens, features), q.dtype),
            pltpu.SemaphoreType.DMA((CHUNKS * heads // group,)),
        ],
        cost_estimate=pl.CostEstimate(
            flops=6 * pairs * HD,
            bytes_accessed=16 * tokens * heads * HD * 2,
            transcendentals=pairs,
        ),
        compiler_params=pltpu.CompilerParams(vmem_limit_bytes=GRANT),
        name="final",
    )(*args)


def prepare_kernel(widths, rows, band_total, width_tiles, col_count, mask, info, q, k, v, *refs):
    near, later = refs[:CHUNKS], refs[CHUNKS : 2 * CHUNKS]
    cand, own, sems = refs[2 * CHUNKS :]
    tokens = q.shape[0]
    wide = widths[0]
    pairs = []
    at = pl.ds(pl.multiple_of(info[1] * rows, rows), rows)
    pairs += [(k.at[at], cand.at[:rows]), (v.at[at], cand.at[rows:])]
    for c in range(CHUNKS):
        part = slice(c * wide, (c + 1) * wide)
        pairs += [(k.at[:, part], near[c].at[:tokens]), (v.at[:, part], near[c].at[tokens:])]
    for c in range(CHUNKS):
        part = slice(c * wide, (c + 1) * wide)
        pairs.append((q.at[:, part], later[c].at[:, :wide]))
    copies = [pltpu.make_async_copy(x, y, sems.at[i]) for i, (x, y) in enumerate(pairs)]
    for copy in copies:
        copy.start()

    band = info[0]
    core = 1 - 2 * lax.rem(band, 2)
    lane = lax.broadcasted_iota(jnp.int32, (tokens, AUX), 1)
    token = lax.broadcasted_iota(jnp.int32, (tokens, AUX), 0)
    tile = lax.rem(token, col_count) // TC
    for slot in range(2):
        full = jnp.zeros((tokens, AUX), jnp.float32)
        for j, dh in enumerate((0, core, -core)):
            inside = (band + dh >= 0) & (band + dh < band_total)
            for cq in range(width_tiles):
                for ck in range(max(0, cq - 1), min(width_tiles, cq + 2)):
                    code = slot * 9 + (dh + 1) * 3 + ck - cq + 1
                    kept = mask[cq, code] > 0
                    if slot == 1 and j == 0 and ck == cq:
                        kept = True
                    value = jnp.where(inside & kept, 1.0, 0.0)
                    hit = (lane == j * width_tiles + ck) & (tile == cq)
                    full = jnp.where(hit, value, full)
        full = full.astype(jnp.bfloat16)
        if slot == 1:
            own[...] = full
        else:
            for c in range(CHUNKS):
                later[c][:, wide:] = full
    for copy in copies:
        copy.wait()


def prepare(q, k, v, mask, info, wide, rows, bands, col_count):
    tokens, features = q.shape
    hbm = pl.BlockSpec(memory_space=pltpu.MemorySpace.HBM)
    smem = pl.BlockSpec(memory_space=pltpu.SMEM)
    vmem = pl.BlockSpec(memory_space=VMEM)
    shapes = [pltpu.VMEM((2 * tokens, wide), q.dtype)] * CHUNKS
    shapes += [pltpu.VMEM((tokens, wide + AUX), q.dtype)] * CHUNKS
    shapes += [pltpu.VMEM((2 * rows, features), q.dtype), pltpu.VMEM((tokens, AUX), q.dtype)]
    args = [pltpu.with_memory_space_constraint(x, pltpu.MemorySpace.HBM) for x in (q, k, v)]
    return pl.pallas_call(
        lambda *refs: prepare_kernel((wide,), rows, bands, mask.shape[0], col_count, *refs),
        in_specs=[smem, smem, hbm, hbm, hbm],
        out_specs=[vmem] * len(shapes),
        out_shape=shapes,
        scratch_shapes=[pltpu.SemaphoreType.DMA((2 + 3 * CHUNKS,))],
        cost_estimate=pl.CostEstimate(
            flops=0, bytes_accessed=16 * tokens * features, transcendentals=0
        ),
        compiler_params=pltpu.CompilerParams(vmem_limit_bytes=GRANT),
        name="prepare",
    )(mask, info, *args)


def swap(x, axis, bit):
    count = lax.axis_size(axis)
    return lax.ppermute(x, axis, [(i, i ^ bit) for i in range(count)])


def shards(queries, keys, values, tile_mask, sink_frame):
    frames, row_count, col_count, features = queries.shape
    tokens = frames * row_count * col_count
    head_count = features // HD
    scale = math.log2(math.e) / math.sqrt(HD)
    times, bands = lax.axis_size("tm"), lax.axis_size("height")
    t, h = lax.axis_index("tm"), lax.axis_index("height")
    assert frames == TF and col_count == 2 * TC and tile_mask.shape[:2] == (1, 1) and head_count % CHUNKS == 0
    assert times & (times - 1) == 0 and bands & (bands - 1) == 0 and bands > 1
    heads = head_count // CHUNKS
    wide = heads * HD
    group = 5 if heads % 5 == 0 else 1

    q, k, v = (x.reshape(tokens, features) for x in (queries, keys, values))

    owner, local = sink_frame[0] // frames, sink_frame[0] % frames
    rows = row_count * col_count
    info = jnp.stack((h, local)).astype(jnp.int32)
    made = prepare(q, k, v, tile_mask[0, 0], info, wide, rows, bands, col_count)
    near_sent, q_sent = made[:CHUNKS], made[CHUNKS : 2 * CHUNKS]
    cand, flags_own = made[2 * CHUNKS :]

    odd = [(i, i + 1) for i in range(1, bands - 1, 2)]
    odd += [(j, i) for i, j in odd]
    sooner = [(i + 1, i) for i in range(times - 1)]
    near = [lax.ppermute(x, "height", odd) for x in near_sent]
    core_k, core_v = swap(k, "height", 1), swap(v, "height", 1)
    q_later = [lax.ppermute(x, "tm", sooner) for x in q_sent]

    bit = 1
    while bit < times:
        other = swap(cand, "tm", bit)
        have = (t ^ owner) // bit == 0
        cand = jnp.where(have, cand, other)
        bit *= 2
    pieces = [cand]
    bit = 2
    while bit < bands:
        pieces += [swap(x, "height", bit) for x in pieces]
        bit *= 2
    twins = [swap(x, "height", 1) for x in pieces]

    states, got = [], []
    for c in range(CHUNKS):
        bands_c = [(k, v, 0, 0, False), (core_k, core_v, 0, 0, False), (near[c], near[c], 0, 1, True)]
        (pay,) = attend(c, heads, group, scale, q_later[c], True, q_later[c], bands_c, False)
        got.append(lax.ppermute(pay, "tm", [(j, i) for i, j in sooner]))
        states.append(attend(c, heads, group, scale, q, False, flags_own, bands_c, True))
    first = (t > 0).astype(jnp.int32).reshape(1)
    early = max(1, len(pieces) - 1)
    *accs, stat = merge_call(heads, group, scale, q, pieces[:early] + twins[:early], states)
    out = final_call(heads, group, scale, q, accs, stat, got, first, pieces[early:] + twins[early:])
    return out.reshape(queries.shape)


def solution(mesh):
    spec = P("tm", "height", None, None)
    return jax.shard_map(
        shards,
        mesh=mesh,
        in_specs=(spec, spec, spec, spec, P()),
        out_specs=spec,
        check_vma=False,
    )
```

```python
import math

import jax
import jax.numpy as jnp
from jax import lax
from jax.experimental import pallas as pl
from jax.experimental.pallas import tpu as pltpu
from jax.sharding import PartitionSpec as P


HD = 128
TF = 4
TC = 8
CHUNKS = 2
NEG = -1e30
AUX = 128
GRANT = 12 << 20


def split3(x):
    hi = x.astype(jnp.bfloat16).astype(jnp.float32)
    mid = (x - hi).astype(jnp.bfloat16).astype(jnp.float32)
    return hi, mid, x - hi - mid


def dot(x, y, contract):
    dims = (((contract,), (contract,)), ((), ()))
    return lax.dot_general(x, y, dims, preferred_element_type=jnp.float32)


VMEM = pltpu.MemorySpace.VMEM


def near_core(x):
    return pltpu.with_memory_space_constraint(x, VMEM)


def lanes(head):
    return pl.ds(pl.multiple_of(head * HD, HD), HD)


def attend_kernel(chunk, heads, group, scale, places, n_arrays, own, *refs):
    arrays = refs[:n_arrays]
    q, q_part = arrays[0], not own
    flags = arrays[1] if own else q
    acc, stat, bias = refs[n_arrays:]
    tokens = q.shape[0]
    pad = stat.shape[0] // 2

    second = (lax.broadcasted_iota(jnp.int32, (tokens, tokens), 0) // TC) % 2 == 1
    kept = jnp.where(flags[:, flags.shape[1] - AUX :].astype(jnp.float32).T > 0.5, 0.0, NEG)
    for j in range(len(places)):
        one = jnp.broadcast_to(kept[2 * j : 2 * j + 1], second.shape)
        two = jnp.broadcast_to(kept[2 * j + 1 : 2 * j + 2], second.shape)
        bias[j * tokens : (j + 1) * tokens] = jnp.where(second, two, one)
    stat[...] = jnp.zeros_like(stat)

    def step(i, _):
        for g in range(group):
            head = i * group + g
            there = lanes(chunk * heads + head)
            here = lanes(head)

            def block(n, row, part):
                return arrays[n][row * tokens : (row + 1) * tokens, here if part else there]

            k = jnp.concatenate([block(nk, rk, part) for nk, rk, _, _, part in places], axis=0)
            v = jnp.concatenate([block(nv, rv, part) for _, _, nv, rv, part in places], axis=0)
            s = dot(k, q[:, here if q_part else there], 1) * scale + bias[...]
            m = jnp.max(s, axis=0, keepdims=True)
            p = jnp.exp2(s - m).astype(jnp.bfloat16)
            acc[here] = dot(v, p, 0).astype(acc.dtype)
            stat[pl.ds(head, 1)] = m
            stat[pl.ds(pad + head, 1)] = jnp.sum(p.astype(jnp.float32), axis=0, keepdims=True)
        return 0

    lax.fori_loop(0, heads // group, step, 0)
    if not own:
        parts = split3(stat[:pad]) + split3(stat[pad:])[:2]
        for i, part in enumerate(parts):
            acc[heads * HD + i * pad : heads * HD + (i + 1) * pad] = part.astype(acc.dtype)


def padded(heads):
    return -(-heads // 16) * 16


def attend(chunk, heads, group, scale, q, flags, bands):
    tokens, pad = q.shape[0], padded(heads)
    own = flags is not None
    args = [q, flags] if own else [q]
    places = []
    for k, rk, v, rv, part in bands:
        where = []
        for x in (k, v):
            if not any(x is y for y in args):
                args.append(x)
            where.append([x is y for y in args].index(True))
        places.append((where[0], rk, where[1], rv, part))
    keys = len(bands) * tokens
    stat = (2 * pad, tokens)
    vmem = pl.BlockSpec(memory_space=VMEM)
    if own:
        out_shape = (pltpu.VMEM((heads * HD, tokens), jnp.float32), pltpu.VMEM(stat, jnp.float32))
        scratch = []
    else:
        out_shape = (pltpu.VMEM((heads * HD + 5 * pad, tokens), jnp.bfloat16),)
        scratch = [pltpu.VMEM(stat, jnp.float32)]
    pairs = tokens * keys * heads
    return pl.pallas_call(
        lambda *refs: attend_kernel(chunk, heads, group, scale, places, len(args), own, *refs),
        in_specs=[vmem] * len(args),
        out_specs=(vmem,) * len(out_shape),
        out_shape=out_shape,
        scratch_shapes=scratch + [pltpu.VMEM((keys, tokens), jnp.float32)],
        cost_estimate=pl.CostEstimate(
            flops=6 * pairs * HD, bytes_accessed=10 * tokens * heads * HD * 2, transcendentals=pairs
        ),
        compiler_params=pltpu.CompilerParams(vmem_limit_bytes=GRANT),
        name="attend",
    )(*[near_core(x) for x in args])


def final_kernel(heads, group, scale, n_sink, *refs):
    q = refs[0]
    accs, stats, gots = (refs[1 + i * CHUNKS :][:CHUNKS] for i in range(3))
    pieces = refs[1 + 3 * CHUNKS : 1 + 3 * CHUNKS + n_sink]
    rows = pieces[0].shape[0] // 2
    out, state, done, sems = refs[-4:]
    pad = padded(heads)
    wide = group * HD
    turns = heads // group

    def copy(turn):
        at = pl.ds(pl.multiple_of(turn * wide, HD), wide)
        return pltpu.make_async_copy(done.at[:, at], out.at[:, at], sems.at[turn])

    for c in range(CHUNKS):
        got = gots[c]
        part = [
            got[heads * HD + i * pad : heads * HD + (i + 1) * pad].astype(jnp.float32)
            for i in range(5)
        ]
        m1, l1 = stats[c][:pad], stats[c][pad:]
        l2 = part[3] + part[4]
        m2 = jnp.where(l2 > 0, part[0] + part[1] + part[2], NEG)
        m12 = jnp.maximum(m1, m2)
        e1, e2 = jnp.exp2(m1 - m12), jnp.exp2(m2 - m12)
        for i, x in enumerate((m12, e1, e2, e1 * l1 + e2 * l2)):
            state[i * pad : (i + 1) * pad] = x

        def step(i, _):
            for g in range(group):
                head = i * group + g
                there, here = lanes(c * heads + head), lanes(head)
                m12, e1, e2, l12 = (state[pl.ds(n * pad + head, 1)] for n in range(4))
                k = jnp.concatenate([r[:rows, there] for r in pieces], axis=0)
                v = jnp.concatenate([r[rows:, there] for r in pieces], axis=0)
                s = dot(k, q[:, there], 1) * scale
                top = jnp.maximum(jnp.max(s, axis=0, keepdims=True), m12)
                p = jnp.exp2(s - top).astype(jnp.bfloat16)
                f = jnp.exp2(m12 - top)
                den = jnp.sum(p.astype(jnp.float32), axis=0, keepdims=True) + f * l12
                inv = 1.0 / den
                theirs = got[here].astype(jnp.float32)
                res = dot(v, p, 0) * inv + accs[c][here] * (f * e1 * inv) + theirs * (f * e2 * inv)
                done[:, there] = res.T.astype(done.dtype)
            copy(c * turns + i).start()
            return 0

        lax.fori_loop(0, turns, step, 0)

    def end(i, _):
        copy(i).wait()
        return 0

    lax.fori_loop(0, CHUNKS * turns, end, 0)


def final_call(heads, group, scale, q, states, gots, pieces):
    tokens, features = q.shape
    args = [q, *[s[0] for s in states], *[s[1] for s in states], *gots, *pieces]
    vmem = pl.BlockSpec(memory_space=VMEM)
    specs = [vmem] * len(args)
    args = [near_core(x) for x in args]
    pairs = tokens * sum(x.shape[0] for x in pieces) // 2 * heads * CHUNKS
    return pl.pallas_call(
        lambda *refs: final_kernel(heads, group, scale, len(pieces), *refs),
        in_specs=specs,
        out_specs=pl.BlockSpec(memory_space=pltpu.MemorySpace.HBM),
        out_shape=jax.ShapeDtypeStruct((tokens, features), q.dtype),
        scratch_shapes=[
            pltpu.VMEM((4 * padded(heads), tokens), jnp.float32),
            pltpu.VMEM((tokens, features), q.dtype),
            pltpu.SemaphoreType.DMA((CHUNKS * heads // group,)),
        ],
        cost_estimate=pl.CostEstimate(
            flops=6 * pairs * HD,
            bytes_accessed=16 * tokens * heads * HD * 2,
            transcendentals=pairs,
        ),
        compiler_params=pltpu.CompilerParams(vmem_limit_bytes=GRANT),
        name="final",
    )(*args)


def copy_all(pairs, sems):
    copies = [pltpu.make_async_copy(x, y, sems.at[i]) for i, (x, y) in enumerate(pairs)]
    for copy in copies:
        copy.start()
    return copies


def part(c, wide):
    return slice(c * wide, (c + 1) * wide)


def sink_kernel(rows, wide, info, k, v, cand, near, sems):
    tokens = k.shape[0]
    at = pl.ds(pl.multiple_of(info[0] * rows, rows), rows)
    pairs = [(k.at[at], cand.at[:rows]), (v.at[at], cand.at[rows:])]
    pairs += [(k.at[:, :wide], near.at[:tokens]), (v.at[:, :wide], near.at[tokens:])]
    for copy in copy_all(pairs, sems):
        copy.wait()


def later_kernel(wide, band_total, width_tiles, col_count, mask, info, q, k, v, *refs):
    near, later = refs[: CHUNKS - 1], refs[CHUNKS - 1 : 2 * CHUNKS - 1]
    own, sems = refs[2 * CHUNKS - 1 :]
    tokens = q.shape[0]
    pairs = [(q.at[:, part(c, wide)], later[c].at[:, :wide]) for c in range(CHUNKS)]
    for c in range(1, CHUNKS):
        pairs += [(k.at[:, part(c, wide)], near[c - 1].at[:tokens])]
        pairs += [(v.at[:, part(c, wide)], near[c - 1].at[tokens:])]
    copies = copy_all(pairs, sems)

    band = info[1]
    core = 1 - 2 * lax.rem(band, 2)
    lane = lax.broadcasted_iota(jnp.int32, (tokens, AUX), 1)
    token = lax.broadcasted_iota(jnp.int32, (tokens, AUX), 0)
    tile = lax.rem(token, col_count) // TC
    for slot in range(2):
        full = jnp.zeros((tokens, AUX), jnp.float32)
        for j, dh in enumerate((0, core, -core)):
            inside = (band + dh >= 0) & (band + dh < band_total)
            for cq in range(width_tiles):
                for ck in range(max(0, cq - 1), min(width_tiles, cq + 2)):
                    code = slot * 9 + (dh + 1) * 3 + ck - cq + 1
                    kept = mask[0, 0, cq, code] > 0
                    if slot == 1 and j == 0 and ck == cq:
                        kept = True
                    value = jnp.where(inside & kept, 1.0, 0.0)
                    hit = (lane == j * width_tiles + ck) & (tile == cq)
                    full = jnp.where(hit, value, full)
        full = full.astype(jnp.bfloat16)
        if slot == 1:
            own[...] = full
        else:
            for c in range(CHUNKS):
                later[c][:, wide:] = full
    for copy in copies:
        copy.wait()


def prepare(q, k, v, mask, info, wide, rows, bands, col_count):
    tokens, features = q.shape
    hbm = pl.BlockSpec(memory_space=pltpu.MemorySpace.HBM)
    smem = pl.BlockSpec(memory_space=pltpu.SMEM)
    vmem = pl.BlockSpec(memory_space=VMEM)
    q, k, v = (pltpu.with_memory_space_constraint(x, pltpu.MemorySpace.HBM) for x in (q, k, v))
    params = pltpu.CompilerParams(vmem_limit_bytes=GRANT)
    near_shape = pltpu.VMEM((2 * tokens, wide), q.dtype)
    cand, near0 = pl.pallas_call(
        lambda *refs: sink_kernel(rows, wide, *refs),
        in_specs=[smem, hbm, hbm],
        out_specs=[vmem] * 2,
        out_shape=[pltpu.VMEM((2 * rows, features), q.dtype), near_shape],
        scratch_shapes=[pltpu.SemaphoreType.DMA((4,))],
        cost_estimate=pl.CostEstimate(
            flops=0, bytes_accessed=8 * tokens * wide, transcendentals=0
        ),
        compiler_params=params,
        name="sink",
    )(info, k, v)
    shapes = [near_shape] * (CHUNKS - 1)
    shapes += [pltpu.VMEM((tokens, wide + AUX), q.dtype)] * CHUNKS
    shapes.append(pltpu.VMEM((tokens, AUX), q.dtype))
    made = pl.pallas_call(
        lambda *refs: later_kernel(wide, bands, mask.shape[2], col_count, *refs),
        in_specs=[smem, smem, hbm, hbm, hbm],
        out_specs=[vmem] * len(shapes),
        out_shape=shapes,
        scratch_shapes=[pltpu.SemaphoreType.DMA((3 * CHUNKS - 2,))],
        cost_estimate=pl.CostEstimate(
            flops=0, bytes_accessed=12 * tokens * features, transcendentals=0
        ),
        compiler_params=params,
        name="later",
    )(mask, info, q, k, v)
    return cand, [near0, *made[: CHUNKS - 1]], made[CHUNKS - 1 : -1], made[-1]


def choose(mine, other, info, bit):
    def body(info, x, y, out):
        @pl.when(info[2] < bit)
        def _():
            out[...] = x[...]

        @pl.when(info[2] >= bit)
        def _():
            out[...] = y[...]

    vmem = pl.BlockSpec(memory_space=VMEM)
    return pl.pallas_call(
        body,
        in_specs=[pl.BlockSpec(memory_space=pltpu.SMEM), vmem, vmem],
        out_specs=vmem,
        out_shape=pltpu.VMEM(mine.shape, mine.dtype),
        cost_estimate=pl.CostEstimate(flops=0, bytes_accessed=4 * mine.size, transcendentals=0),
        compiler_params=pltpu.CompilerParams(vmem_limit_bytes=GRANT),
        name="choose",
    )(info, near_core(mine), near_core(other))


def swap(x, axis, bit):
    count = lax.axis_size(axis)
    return lax.ppermute(x, axis, [(i, i ^ bit) for i in range(count)])


def shards(queries, keys, values, tile_mask, sink_frame):
    frames, row_count, col_count, features = queries.shape
    tokens = frames * row_count * col_count
    head_count = features // HD
    scale = math.log2(math.e) / math.sqrt(HD)
    times, bands = lax.axis_size("tm"), lax.axis_size("height")
    t, h = lax.axis_index("tm"), lax.axis_index("height")
    assert frames == TF and col_count == 2 * TC and tile_mask.shape[:2] == (1, 1) and head_count % CHUNKS == 0
    assert times & (times - 1) == 0 and bands & (bands - 1) == 0 and bands > 1
    heads = head_count // CHUNKS
    wide = heads * HD
    group = heads

    q, k, v = (x.reshape(tokens, features) for x in (queries, keys, values))

    owner, local = sink_frame[0] // frames, sink_frame[0] % frames
    rows = row_count * col_count
    info = jnp.stack((local, h, t ^ owner)).astype(jnp.int32)
    cand, near_sent, q_sent, flags_own = prepare(
        q, k, v, tile_mask, info, wide, rows, bands, col_count
    )

    odd = [(i, i + 1) for i in range(1, bands - 1, 2)]
    odd += [(j, i) for i, j in odd]
    sooner = [(i + 1, i) for i in range(times - 1)]
    near = [lax.ppermute(x, "height", odd) for x in near_sent]
    core_k, core_v = swap(k, "height", 1), swap(v, "height", 1)
    q_later = [lax.ppermute(x, "tm", sooner) for x in q_sent]

    bit = 1
    while bit < times:
        other = swap(cand, "tm", bit)
        cand = choose(cand, other, info, bit)
        bit *= 2
    pieces = [cand]
    bit = 2
    while bit < bands:
        pieces += [swap(x, "height", bit) for x in pieces]
        bit *= 2
    twins = [swap(x, "height", 1) for x in pieces]

    states, got = [], []
    for c in range(CHUNKS):
        bands_c = [(k, 0, v, 0, False), (core_k, 0, core_v, 0, False), (near[c], 0, near[c], 1, True)]
        (pay,) = attend(c, heads, group, scale, q_later[c], None, bands_c)
        got.append(lax.ppermute(pay, "tm", [(j, i) for i, j in sooner]))
        states.append(attend(c, heads, group, scale, q, flags_own, bands_c))
    out = final_call(heads, group, scale, q, states, got, pieces + twins)
    return out.reshape(queries.shape)


def solution(mesh):
    spec = P("tm", "height", None, None)
    return jax.shard_map(
        shards,
        mesh=mesh,
        in_specs=(spec, spec, spec, spec, P()),
        out_specs=spec,
        check_vma=False,
    )
```

```python
import math

import jax
import jax.numpy as jnp
from jax import lax
from jax.experimental import pallas as pl
from jax.experimental.pallas import tpu as pltpu
from jax.sharding import PartitionSpec as P


HD = 128
TF = 4
TC = 8
CHUNKS = 2
NEG = -1e30
AUX = 128
GRANT = 12 << 20


def split3(x):
    hi = x.astype(jnp.bfloat16).astype(jnp.float32)
    mid = (x - hi).astype(jnp.bfloat16).astype(jnp.float32)
    return hi, mid, x - hi - mid


def dot(x, y, contract):
    dims = (((contract,), (contract,)), ((), ()))
    return lax.dot_general(x, y, dims, preferred_element_type=jnp.float32)


VMEM = pltpu.MemorySpace.VMEM


def near_core(x):
    return pltpu.with_memory_space_constraint(x, VMEM)


def lanes(head):
    return pl.ds(pl.multiple_of(head * HD, HD), HD)


def attend_kernel(chunk, heads, group, scale, places, n_arrays, own, *refs):
    arrays = refs[:n_arrays]
    q, q_part = arrays[0], not own
    flags = arrays[1] if own else q
    acc, stat, bias = refs[n_arrays:]
    tokens = q.shape[0]
    pad = stat.shape[0] // 2

    second = (lax.broadcasted_iota(jnp.int32, (tokens, tokens), 0) // TC) % 2 == 1
    kept = jnp.where(flags[:, flags.shape[1] - AUX :].astype(jnp.float32).T > 0.5, 0.0, NEG)
    for j in range(len(places)):
        one = jnp.broadcast_to(kept[2 * j : 2 * j + 1], second.shape)
        two = jnp.broadcast_to(kept[2 * j + 1 : 2 * j + 2], second.shape)
        bias[j * tokens : (j + 1) * tokens] = jnp.where(second, two, one)
    stat[...] = jnp.zeros_like(stat)

    def step(i, _):
        for g in range(group):
            head = i * group + g
            there = lanes(chunk * heads + head)
            here = lanes(head)

            def block(n, row, part):
                return arrays[n][row * tokens : (row + 1) * tokens, here if part else there]

            k = jnp.concatenate([block(nk, rk, part) for nk, rk, _, _, part in places], axis=0)
            v = jnp.concatenate([block(nv, rv, part) for _, _, nv, rv, part in places], axis=0)
            s = dot(k, q[:, here if q_part else there], 1) * scale + bias[...]
            m = jnp.max(s, axis=0, keepdims=True)
            p = jnp.exp2(s - m).astype(jnp.bfloat16)
            acc[here] = dot(v, p, 0).astype(acc.dtype)
            stat[pl.ds(head, 1)] = m
            stat[pl.ds(pad + head, 1)] = jnp.sum(p.astype(jnp.float32), axis=0, keepdims=True)
        return 0

    lax.fori_loop(0, heads // group, step, 0)
    if not own:
        parts = split3(stat[:pad]) + split3(stat[pad:])[:2]
        for i, part in enumerate(parts):
            acc[heads * HD + i * pad : heads * HD + (i + 1) * pad] = part.astype(acc.dtype)


def padded(heads):
    return -(-heads // 16) * 16


def attend(chunk, heads, group, scale, q, flags, bands):
    tokens, pad = q.shape[0], padded(heads)
    own = flags is not None
    args = [q, flags] if own else [q]
    places = []
    for k, rk, v, rv, part in bands:
        where = []
        for x in (k, v):
            if not any(x is y for y in args):
                args.append(x)
            where.append([x is y for y in args].index(True))
        places.append((where[0], rk, where[1], rv, part))
    keys = len(bands) * tokens
    stat = (2 * pad, tokens)
    vmem = pl.BlockSpec(memory_space=VMEM)
    if own:
        out_shape = (pltpu.VMEM((heads * HD, tokens), jnp.float32), pltpu.VMEM(stat, jnp.float32))
        scratch = []
    else:
        out_shape = (pltpu.VMEM((heads * HD + 5 * pad, tokens), jnp.bfloat16),)
        scratch = [pltpu.VMEM(stat, jnp.float32)]
    pairs = tokens * keys * heads
    return pl.pallas_call(
        lambda *refs: attend_kernel(chunk, heads, group, scale, places, len(args), own, *refs),
        in_specs=[vmem] * len(args),
        out_specs=(vmem,) * len(out_shape),
        out_shape=out_shape,
        scratch_shapes=scratch + [pltpu.VMEM((keys, tokens), jnp.float32)],
        cost_estimate=pl.CostEstimate(
            flops=6 * pairs * HD, bytes_accessed=10 * tokens * heads * HD * 2, transcendentals=pairs
        ),
        compiler_params=pltpu.CompilerParams(vmem_limit_bytes=GRANT),
        name="attend",
    )(*[near_core(x) for x in args])


def final_kernel(heads, cut, scale, n_sink, *refs):
    q = refs[0]
    accs, stats, gots = (refs[1 + i * CHUNKS :][:CHUNKS] for i in range(3))
    pieces = [refs[1 + 3 * CHUNKS + c * n_sink :][:n_sink] for c in range(CHUNKS)]
    rows = pieces[0][0].shape[0] // 2
    out, done, sems = refs[-3:]
    pad = padded(heads)
    copies = []
    for c in range(CHUNKS):
        got = gots[c]
        part = [
            got[heads * HD + i * pad : heads * HD + (i + 1) * pad].astype(jnp.float32)
            for i in range(5)
        ]
        m1, l1 = stats[c][:pad], stats[c][pad:]
        l2 = part[3] + part[4]
        m2 = jnp.where(l2 > 0, part[0] + part[1] + part[2], NEG)
        m12 = jnp.maximum(m1, m2)
        e1, e2 = jnp.exp2(m1 - m12), jnp.exp2(m2 - m12)
        l12 = e1 * l1 + e2 * l2
        for head in range(heads):
            one, here = slice(head, head + 1), slice(head * HD, (head + 1) * HD)
            at = (c * heads + head) * HD
            there = slice(at, at + HD)
            k = jnp.concatenate([r[:rows, here] for r in pieces[c]], axis=0)
            v = jnp.concatenate([r[rows:, here] for r in pieces[c]], axis=0)
            s = dot(k, q[:, there], 1) * scale
            top = jnp.maximum(jnp.max(s, axis=0, keepdims=True), m12[one])
            p = jnp.exp2(s - top).astype(jnp.bfloat16)
            f = jnp.exp2(m12[one] - top)
            inv = 1.0 / (jnp.sum(p.astype(jnp.float32), axis=0, keepdims=True) + f * l12[one])
            theirs = got[here].astype(jnp.float32)
            mine = accs[c][here] * (f * e1[one] * inv)
            res = dot(v, p, 0) * inv + mine + theirs * (f * e2[one] * inv)
            done[:, there] = res.T.astype(done.dtype)
            if (c * heads + head + 1) % cut == 0:
                cols = pl.ds(at + HD - cut * HD, cut * HD)
                copies.append(
                    pltpu.make_async_copy(done.at[:, cols], out.at[:, cols], sems.at[len(copies)])
                )
                copies[-1].start()
    for copy in copies:
        copy.wait()


def final_call(heads, scale, q, states, gots, pieces):
    tokens, features = q.shape
    cut = math.gcd(CHUNKS * heads, 5)
    args = [q, *[s[0] for s in states], *[s[1] for s in states], *gots, *[x for p in pieces for x in p]]
    vmem = pl.BlockSpec(memory_space=VMEM)
    specs = [vmem] * len(args)
    args = [near_core(x) for x in args]
    pairs = tokens * sum(x.shape[0] for x in pieces[0]) // 2 * heads * CHUNKS
    return pl.pallas_call(
        lambda *refs: final_kernel(heads, cut, scale, len(pieces[0]), *refs),
        in_specs=specs,
        out_specs=pl.BlockSpec(memory_space=pltpu.MemorySpace.HBM),
        out_shape=jax.ShapeDtypeStruct((tokens, features), q.dtype),
        scratch_shapes=[
            pltpu.VMEM((tokens, features), q.dtype),
            pltpu.SemaphoreType.DMA((CHUNKS * heads // cut,)),
        ],
        cost_estimate=pl.CostEstimate(
            flops=6 * pairs * HD,
            bytes_accessed=16 * tokens * heads * HD * 2,
            transcendentals=pairs,
        ),
        compiler_params=pltpu.CompilerParams(vmem_limit_bytes=GRANT),
        name="final",
    )(*args)


def copy_all(pairs, sems):
    copies = [pltpu.make_async_copy(x, y, sems.at[i]) for i, (x, y) in enumerate(pairs)]
    for copy in copies:
        copy.start()
    return copies


def part(c, wide):
    return slice(c * wide, (c + 1) * wide)


def sink_kernel(rows, wide, info, k, v, cand, near, sems):
    tokens = k.shape[0]
    at = pl.ds(pl.multiple_of(info[0] * rows, rows), rows)
    pairs = [(k.at[at], cand.at[:rows]), (v.at[at], cand.at[rows:])]
    pairs += [(k.at[:, :wide], near.at[:tokens]), (v.at[:, :wide], near.at[tokens:])]
    for copy in copy_all(pairs, sems):
        copy.wait()


def later_kernel(wide, band_total, width_tiles, col_count, mask, info, q, k, v, *refs):
    near, later = refs[: CHUNKS - 1], refs[CHUNKS - 1 : 2 * CHUNKS - 1]
    own, sems = refs[2 * CHUNKS - 1 :]
    tokens = q.shape[0]
    pairs = [(q.at[:, part(c, wide)], later[c].at[:, :wide]) for c in range(CHUNKS)]
    for c in range(1, CHUNKS):
        pairs += [(k.at[:, part(c, wide)], near[c - 1].at[:tokens])]
        pairs += [(v.at[:, part(c, wide)], near[c - 1].at[tokens:])]
    copies = copy_all(pairs, sems)

    band = info[1]
    core = 1 - 2 * lax.rem(band, 2)
    lane = lax.broadcasted_iota(jnp.int32, (tokens, AUX), 1)
    token = lax.broadcasted_iota(jnp.int32, (tokens, AUX), 0)
    tile = lax.rem(token, col_count) // TC
    for slot in range(2):
        full = jnp.zeros((tokens, AUX), jnp.float32)
        for j, dh in enumerate((0, core, -core)):
            inside = (band + dh >= 0) & (band + dh < band_total)
            for cq in range(width_tiles):
                for ck in range(max(0, cq - 1), min(width_tiles, cq + 2)):
                    code = slot * 9 + (dh + 1) * 3 + ck - cq + 1
                    kept = mask[0, 0, cq, code] > 0
                    if slot == 1 and j == 0 and ck == cq:
                        kept = True
                    value = jnp.where(inside & kept, 1.0, 0.0)
                    hit = (lane == j * width_tiles + ck) & (tile == cq)
                    full = jnp.where(hit, value, full)
        full = full.astype(jnp.bfloat16)
        if slot == 1:
            own[...] = full
        else:
            for c in range(CHUNKS):
                later[c][:, wide:] = full
    for copy in copies:
        copy.wait()


def prepare(q, k, v, mask, info, wide, rows, bands, col_count):
    tokens, features = q.shape
    hbm = pl.BlockSpec(memory_space=pltpu.MemorySpace.HBM)
    smem = pl.BlockSpec(memory_space=pltpu.SMEM)
    vmem = pl.BlockSpec(memory_space=VMEM)
    q, k, v = (pltpu.with_memory_space_constraint(x, pltpu.MemorySpace.HBM) for x in (q, k, v))
    params = pltpu.CompilerParams(vmem_limit_bytes=GRANT)
    near_shape = pltpu.VMEM((2 * tokens, wide), q.dtype)
    cand, near0 = pl.pallas_call(
        lambda *refs: sink_kernel(rows, wide, *refs),
        in_specs=[smem, hbm, hbm],
        out_specs=[vmem] * 2,
        out_shape=[pltpu.VMEM((2 * rows, features), q.dtype), near_shape],
        scratch_shapes=[pltpu.SemaphoreType.DMA((4,))],
        cost_estimate=pl.CostEstimate(
            flops=0, bytes_accessed=8 * tokens * wide, transcendentals=0
        ),
        compiler_params=params,
        name="sink",
    )(info, k, v)
    shapes = [near_shape] * (CHUNKS - 1)
    shapes += [pltpu.VMEM((tokens, wide + AUX), q.dtype)] * CHUNKS
    shapes.append(pltpu.VMEM((tokens, AUX), q.dtype))
    made = pl.pallas_call(
        lambda *refs: later_kernel(wide, bands, mask.shape[2], col_count, *refs),
        in_specs=[smem, smem, hbm, hbm, hbm],
        out_specs=[vmem] * len(shapes),
        out_shape=shapes,
        scratch_shapes=[pltpu.SemaphoreType.DMA((3 * CHUNKS - 2,))],
        cost_estimate=pl.CostEstimate(
            flops=0, bytes_accessed=12 * tokens * features, transcendentals=0
        ),
        compiler_params=params,
        name="later",
    )(mask, info, q, k, v)
    return cand, [near0, *made[: CHUNKS - 1]], made[CHUNKS - 1 : -1], made[-1]


def choose(mine, other, info, bit, parts):
    wide = mine.shape[1] // parts

    def body(info, x, y, *outs):
        @pl.when(info[2] < bit)
        def _():
            for i, out in enumerate(outs):
                out[...] = x[:, part(i, wide)]

        @pl.when(info[2] >= bit)
        def _():
            for i, out in enumerate(outs):
                out[...] = y[:, part(i, wide)]

    vmem = pl.BlockSpec(memory_space=VMEM)
    return pl.pallas_call(
        body,
        in_specs=[pl.BlockSpec(memory_space=pltpu.SMEM), vmem, vmem],
        out_specs=[vmem] * parts,
        out_shape=[pltpu.VMEM((mine.shape[0], wide), mine.dtype)] * parts,
        cost_estimate=pl.CostEstimate(flops=0, bytes_accessed=4 * mine.size, transcendentals=0),
        compiler_params=pltpu.CompilerParams(vmem_limit_bytes=GRANT),
        name="choose",
    )(info, near_core(mine), near_core(other))


def swap(x, axis, bit):
    count = lax.axis_size(axis)
    return lax.ppermute(x, axis, [(i, i ^ bit) for i in range(count)])


def shards(queries, keys, values, tile_mask, sink_frame):
    frames, row_count, col_count, features = queries.shape
    tokens = frames * row_count * col_count
    head_count = features // HD
    scale = math.log2(math.e) / math.sqrt(HD)
    times, bands = lax.axis_size("tm"), lax.axis_size("height")
    t, h = lax.axis_index("tm"), lax.axis_index("height")
    assert frames == TF and col_count == 2 * TC and tile_mask.shape[:2] == (1, 1) and head_count % CHUNKS == 0
    assert times & (times - 1) == 0 and bands & (bands - 1) == 0 and min(times, bands) > 1
    heads = head_count // CHUNKS
    wide = heads * HD
    group = heads

    q, k, v = (x.reshape(tokens, features) for x in (queries, keys, values))

    owner, local = sink_frame[0] // frames, sink_frame[0] % frames
    rows = row_count * col_count
    info = jnp.stack((local, h, t ^ owner)).astype(jnp.int32)
    cand, near_sent, q_sent, flags_own = prepare(
        q, k, v, tile_mask, info, wide, rows, bands, col_count
    )

    odd = [(i, i + 1) for i in range(1, bands - 1, 2)]
    odd += [(j, i) for i, j in odd]
    sooner = [(i + 1, i) for i in range(times - 1)]
    near = [lax.ppermute(x, "height", odd) for x in near_sent]
    core_k, core_v = swap(k, "height", 1), swap(v, "height", 1)
    q_later = [lax.ppermute(x, "tm", sooner) for x in q_sent]

    parts = choose(cand, swap(cand, "tm", 1), info, 1, CHUNKS)
    pieces = []
    for cand in parts:
        bit = 2
        while bit < times:
            other = swap(cand, "tm", bit)
            (cand,) = choose(cand, other, info, bit, 1)
            bit *= 2
        mine = [cand] + [swap(cand, "height", d) for d in range(2, bands, 2)]
        pieces.append(mine + [swap(x, "height", 1) for x in mine])

    states, got = [], []
    for c in range(CHUNKS):
        bands_c = [(k, 0, v, 0, False), (core_k, 0, core_v, 0, False), (near[c], 0, near[c], 1, True)]
        (pay,) = attend(c, heads, group, scale, q_later[c], None, bands_c)
        got.append(lax.ppermute(pay, "tm", [(j, i) for i, j in sooner]))
        states.append(attend(c, heads, group, scale, q, flags_own, bands_c))
    out = final_call(heads, scale, q, states, got, pieces)
    return out.reshape(queries.shape)


def solution(mesh):
    spec = P("tm", "height", None, None)
    return jax.shard_map(
        shards,
        mesh=mesh,
        in_specs=(spec, spec, spec, spec, P()),
        out_specs=spec,
        check_vma=False,
    )
```

```python
import math

import jax
import jax.numpy as jnp
from jax import lax
from jax.experimental import pallas as pl
from jax.experimental.pallas import tpu as pltpu
from jax.sharding import PartitionSpec as P


HD = 128
TF = 4
TC = 8
CHUNKS = 2
LATE = 8
NEG = -1e30
AUX = 128
GRANT = 12 << 20


def split3(x):
    hi = x.astype(jnp.bfloat16).astype(jnp.float32)
    mid = (x - hi).astype(jnp.bfloat16).astype(jnp.float32)
    return hi, mid, x - hi - mid


def dot(x, y, contract):
    dims = (((contract,), (contract,)), ((), ()))
    return lax.dot_general(x, y, dims, preferred_element_type=jnp.float32)


VMEM = pltpu.MemorySpace.VMEM


def near_core(x):
    return pltpu.with_memory_space_constraint(x, VMEM)


def lanes(head):
    return pl.ds(pl.multiple_of(head * HD, HD), HD)


def attend_kernel(first, heads, group, scale, places, n_arrays, own, *refs):
    arrays = refs[:n_arrays]
    q, q_part = arrays[0], not own
    flags = arrays[1] if own else q
    acc, stat, bias = refs[n_arrays:]
    tokens = q.shape[0]
    pad = stat.shape[0] // 2

    second = (lax.broadcasted_iota(jnp.int32, (tokens, tokens), 0) // TC) % 2 == 1
    kept = jnp.where(flags[:, flags.shape[1] - AUX :].astype(jnp.float32).T > 0.5, 0.0, NEG)
    for j in range(len(places)):
        one = jnp.broadcast_to(kept[2 * j : 2 * j + 1], second.shape)
        two = jnp.broadcast_to(kept[2 * j + 1 : 2 * j + 2], second.shape)
        bias[j * tokens : (j + 1) * tokens] = jnp.where(second, two, one)
    stat[...] = jnp.zeros_like(stat)

    def step(i, _):
        for g in range(group):
            head = i * group + g
            there = lanes(first + head)
            here = lanes(head)

            def block(n, row, part):
                return arrays[n][row * tokens : (row + 1) * tokens, here if part else there]

            k = jnp.concatenate([block(nk, rk, part) for nk, rk, _, _, part in places], axis=0)
            v = jnp.concatenate([block(nv, rv, part) for _, _, nv, rv, part in places], axis=0)
            s = dot(k, q[:, here if q_part else there], 1) * scale + bias[...]
            m = jnp.max(s, axis=0, keepdims=True)
            p = jnp.exp2(s - m).astype(jnp.bfloat16)
            acc[here] = dot(v, p, 0).astype(acc.dtype)
            stat[pl.ds(head, 1)] = m
            stat[pl.ds(pad + head, 1)] = jnp.sum(p.astype(jnp.float32), axis=0, keepdims=True)
        return 0

    lax.fori_loop(0, heads // group, step, 0)
    if not own:
        parts = split3(stat[:pad]) + split3(stat[pad:])[:2]
        for i, part in enumerate(parts):
            acc[heads * HD + i * pad : heads * HD + (i + 1) * pad] = part.astype(acc.dtype)


def padded(heads):
    return -(-heads // 16) * 16


def attend(first, heads, scale, q, flags, bands):
    tokens, pad = q.shape[0], padded(heads)
    own = flags is not None
    args = [q, flags] if own else [q]
    places = []
    for k, rk, v, rv, part in bands:
        where = []
        for x in (k, v):
            if not any(x is y for y in args):
                args.append(x)
            where.append([x is y for y in args].index(True))
        places.append((where[0], rk, where[1], rv, part))
    keys = len(bands) * tokens
    stat = (2 * pad, tokens)
    vmem = pl.BlockSpec(memory_space=VMEM)
    if own:
        out_shape = (pltpu.VMEM((heads * HD, tokens), jnp.float32), pltpu.VMEM(stat, jnp.float32))
        scratch = []
    else:
        out_shape = (pltpu.VMEM((heads * HD + 5 * pad, tokens), jnp.bfloat16),)
        scratch = [pltpu.VMEM(stat, jnp.float32)]
    pairs = tokens * keys * heads
    return pl.pallas_call(
        lambda *refs: attend_kernel(first, heads, heads, scale, places, len(args), own, *refs),
        in_specs=[vmem] * len(args),
        out_specs=(vmem,) * len(out_shape),
        out_shape=out_shape,
        scratch_shapes=scratch + [pltpu.VMEM((keys, tokens), jnp.float32)],
        cost_estimate=pl.CostEstimate(
            flops=6 * pairs * HD, bytes_accessed=10 * tokens * heads * HD * 2, transcendentals=pairs
        ),
        compiler_params=pltpu.CompilerParams(vmem_limit_bytes=GRANT),
        name="attend",
    )(*[near_core(x) for x in args])


def final_kernel(counts, cut, scale, n_sink, *refs):
    q = refs[0]
    accs, stats, gots = (refs[1 + i * CHUNKS :][:CHUNKS] for i in range(3))
    pieces = [refs[1 + 3 * CHUNKS + c * n_sink :][:n_sink] for c in range(CHUNKS)]
    rows = pieces[0][0].shape[0] // 2
    out, done, sems = refs[-3:]
    copies = []
    for c, heads in enumerate(counts):
        got, pad = gots[c], padded(heads)
        part = [
            got[heads * HD + i * pad : heads * HD + (i + 1) * pad].astype(jnp.float32)
            for i in range(5)
        ]
        m1, l1 = stats[c][:pad], stats[c][pad:]
        l2 = part[3] + part[4]
        m2 = jnp.where(l2 > 0, part[0] + part[1] + part[2], NEG)
        m12 = jnp.maximum(m1, m2)
        e1, e2 = jnp.exp2(m1 - m12), jnp.exp2(m2 - m12)
        l12 = e1 * l1 + e2 * l2
        for head in range(heads):
            one, here = slice(head, head + 1), slice(head * HD, (head + 1) * HD)
            at = (sum(counts[:c]) + head) * HD
            there = slice(at, at + HD)
            k = jnp.concatenate([r[:rows, here] for r in pieces[c]], axis=0)
            v = jnp.concatenate([r[rows:, here] for r in pieces[c]], axis=0)
            s = dot(k, q[:, there], 1) * scale
            top = jnp.maximum(jnp.max(s, axis=0, keepdims=True), m12[one])
            p = jnp.exp2(s - top).astype(jnp.bfloat16)
            f = jnp.exp2(m12[one] - top)
            inv = 1.0 / (jnp.sum(p.astype(jnp.float32), axis=0, keepdims=True) + f * l12[one])
            theirs = got[here].astype(jnp.float32)
            mine = accs[c][here] * (f * e1[one] * inv)
            res = dot(v, p, 0) * inv + mine + theirs * (f * e2[one] * inv)
            done[:, there] = res.T.astype(done.dtype)
            if (at // HD + 1) % cut == 0:
                cols = pl.ds(at + HD - cut * HD, cut * HD)
                copies.append(
                    pltpu.make_async_copy(done.at[:, cols], out.at[:, cols], sems.at[len(copies)])
                )
                copies[-1].start()
    for copy in copies:
        copy.wait()


def final_call(counts, scale, q, states, gots, pieces):
    tokens, features = q.shape
    cut = math.gcd(sum(counts), 5)
    args = [q, *[s[0] for s in states], *[s[1] for s in states], *gots, *[x for p in pieces for x in p]]
    vmem = pl.BlockSpec(memory_space=VMEM)
    specs = [vmem] * len(args)
    args = [near_core(x) for x in args]
    pairs = tokens * sum(x.shape[0] for x in pieces[0]) // 2 * sum(counts)
    return pl.pallas_call(
        lambda *refs: final_kernel(counts, cut, scale, len(pieces[0]), *refs),
        in_specs=specs,
        out_specs=pl.BlockSpec(memory_space=pltpu.MemorySpace.HBM),
        out_shape=jax.ShapeDtypeStruct((tokens, features), q.dtype),
        scratch_shapes=[
            pltpu.VMEM((tokens, features), q.dtype),
            pltpu.SemaphoreType.DMA((sum(counts) // cut,)),
        ],
        cost_estimate=pl.CostEstimate(
            flops=6 * pairs * HD,
            bytes_accessed=16 * tokens * features,
            transcendentals=pairs,
        ),
        compiler_params=pltpu.CompilerParams(vmem_limit_bytes=GRANT),
        name="final",
    )(*args)


def copy_all(pairs, sems):
    copies = [pltpu.make_async_copy(x, y, sems.at[i]) for i, (x, y) in enumerate(pairs)]
    for copy in copies:
        copy.start()
    return copies


def part(c, widths):
    return slice(sum(widths[:c]), sum(widths[: c + 1]))


def sink_kernel(rows, wide, info, k, v, cand, near, sems):
    tokens = k.shape[0]
    at = pl.ds(pl.multiple_of(info[0] * rows, rows), rows)
    pairs = [(k.at[at], cand.at[:rows]), (v.at[at], cand.at[rows:])]
    pairs += [(k.at[:, :wide], near.at[:tokens]), (v.at[:, :wide], near.at[tokens:])]
    for copy in copy_all(pairs, sems):
        copy.wait()


def later_kernel(widths, band_total, width_tiles, col_count, mask, info, q, k, v, *refs):
    near, later = refs[: CHUNKS - 1], refs[CHUNKS - 1 : 2 * CHUNKS - 1]
    own, sems = refs[2 * CHUNKS - 1 :]
    tokens = q.shape[0]
    pairs = [(q.at[:, part(c, widths)], later[c].at[:, : widths[c]]) for c in range(CHUNKS)]
    for c in range(1, CHUNKS):
        pairs += [(k.at[:, part(c, widths)], near[c - 1].at[:tokens])]
        pairs += [(v.at[:, part(c, widths)], near[c - 1].at[tokens:])]
    copies = copy_all(pairs, sems)

    band = info[1]
    core = 1 - 2 * lax.rem(band, 2)
    lane = lax.broadcasted_iota(jnp.int32, (tokens, AUX), 1)
    token = lax.broadcasted_iota(jnp.int32, (tokens, AUX), 0)
    tile = lax.rem(token, col_count) // TC
    for slot in range(2):
        full = jnp.zeros((tokens, AUX), jnp.float32)
        for j, dh in enumerate((0, core, -core)):
            inside = (band + dh >= 0) & (band + dh < band_total)
            for cq in range(width_tiles):
                for ck in range(max(0, cq - 1), min(width_tiles, cq + 2)):
                    code = slot * 9 + (dh + 1) * 3 + ck - cq + 1
                    kept = mask[0, 0, cq, code] > 0
                    if slot == 1 and j == 0 and ck == cq:
                        kept = True
                    value = jnp.where(inside & kept, 1.0, 0.0)
                    hit = (lane == j * width_tiles + ck) & (tile == cq)
                    full = jnp.where(hit, value, full)
        full = full.astype(jnp.bfloat16)
        if slot == 1:
            own[...] = full
        else:
            for c in range(CHUNKS):
                later[c][:, widths[c] :] = full
    for copy in copies:
        copy.wait()


def prepare(q, k, v, mask, info, widths, rows, bands, col_count):
    tokens, features = q.shape
    hbm = pl.BlockSpec(memory_space=pltpu.MemorySpace.HBM)
    smem = pl.BlockSpec(memory_space=pltpu.SMEM)
    vmem = pl.BlockSpec(memory_space=VMEM)
    q, k, v = (pltpu.with_memory_space_constraint(x, pltpu.MemorySpace.HBM) for x in (q, k, v))
    params = pltpu.CompilerParams(vmem_limit_bytes=GRANT)
    near_shapes = [pltpu.VMEM((2 * tokens, wide), q.dtype) for wide in widths]
    cand, near0 = pl.pallas_call(
        lambda *refs: sink_kernel(rows, widths[0], *refs),
        in_specs=[smem, hbm, hbm],
        out_specs=[vmem] * 2,
        out_shape=[pltpu.VMEM((2 * rows, features), q.dtype), near_shapes[0]],
        scratch_shapes=[pltpu.SemaphoreType.DMA((4,))],
        cost_estimate=pl.CostEstimate(
            flops=0, bytes_accessed=8 * tokens * widths[0], transcendentals=0
        ),
        compiler_params=params,
        name="sink",
    )(info, k, v)
    shapes = near_shapes[1:] + [pltpu.VMEM((tokens, wide + AUX), q.dtype) for wide in widths]
    shapes.append(pltpu.VMEM((tokens, AUX), q.dtype))
    made = pl.pallas_call(
        lambda *refs: later_kernel(widths, bands, mask.shape[2], col_count, *refs),
        in_specs=[smem, smem, hbm, hbm, hbm],
        out_specs=[vmem] * len(shapes),
        out_shape=shapes,
        scratch_shapes=[pltpu.SemaphoreType.DMA((3 * CHUNKS - 2,))],
        cost_estimate=pl.CostEstimate(
            flops=0, bytes_accessed=12 * tokens * features, transcendentals=0
        ),
        compiler_params=params,
        name="later",
    )(mask, info, q, k, v)
    return cand, [near0, *made[: CHUNKS - 1]], made[CHUNKS - 1 : -1], made[-1]


def choose(mine, other, info, bit, widths):
    def body(info, x, y, *outs):
        @pl.when(info[2] < bit)
        def _():
            for i, out in enumerate(outs):
                out[...] = x[:, part(i, widths)]

        @pl.when(info[2] >= bit)
        def _():
            for i, out in enumerate(outs):
                out[...] = y[:, part(i, widths)]

    vmem = pl.BlockSpec(memory_space=VMEM)
    return pl.pallas_call(
        body,
        in_specs=[pl.BlockSpec(memory_space=pltpu.SMEM), vmem, vmem],
        out_specs=[vmem] * len(widths),
        out_shape=[pltpu.VMEM((mine.shape[0], wide), mine.dtype) for wide in widths],
        cost_estimate=pl.CostEstimate(flops=0, bytes_accessed=4 * mine.size, transcendentals=0),
        compiler_params=pltpu.CompilerParams(vmem_limit_bytes=GRANT),
        name="choose",
    )(info, near_core(mine), near_core(other))


def swap(x, axis, bit):
    count = lax.axis_size(axis)
    return lax.ppermute(x, axis, [(i, i ^ bit) for i in range(count)])


def shards(queries, keys, values, tile_mask, sink_frame):
    frames, row_count, col_count, features = queries.shape
    tokens = frames * row_count * col_count
    head_count = features // HD
    scale = math.log2(math.e) / math.sqrt(HD)
    times, bands = lax.axis_size("tm"), lax.axis_size("height")
    t, h = lax.axis_index("tm"), lax.axis_index("height")
    assert frames == TF and col_count == 2 * TC and tile_mask.shape[:2] == (1, 1)
    assert times & (times - 1) == 0 and bands & (bands - 1) == 0 and min(times, bands) > 1
    counts = (head_count - head_count * LATE // 20, head_count * LATE // 20)
    widths = tuple(n * HD for n in counts)

    q, k, v = (x.reshape(tokens, features) for x in (queries, keys, values))

    owner, local = sink_frame[0] // frames, sink_frame[0] % frames
    rows = row_count * col_count
    info = jnp.stack((local, h, t ^ owner)).astype(jnp.int32)
    cand, near_sent, q_sent, flags_own = prepare(
        q, k, v, tile_mask, info, widths, rows, bands, col_count
    )

    odd = [(i, i + 1) for i in range(1, bands - 1, 2)]
    odd += [(j, i) for i, j in odd]
    sooner = [(i + 1, i) for i in range(times - 1)]
    near = [lax.ppermute(x, "height", odd) for x in near_sent]
    core_k, core_v = swap(k, "height", 1), swap(v, "height", 1)
    q_later = [lax.ppermute(x, "tm", sooner) for x in q_sent]

    parts = choose(cand, swap(cand, "tm", 1), info, 1, widths)
    pieces = []
    for c, cand in enumerate(parts):
        bit = 2
        while bit < times:
            other = swap(cand, "tm", bit)
            (cand,) = choose(cand, other, info, bit, widths[c : c + 1])
            bit *= 2
        mine = [cand] + [swap(cand, "height", d) for d in range(2, bands, 2)]
        pieces.append(mine + [swap(x, "height", 1) for x in mine])

    states, got = [], []
    for c in range(CHUNKS):
        first = sum(counts[:c])
        bands_c = [(k, 0, v, 0, False), (core_k, 0, core_v, 0, False), (near[c], 0, near[c], 1, True)]
        (pay,) = attend(first, counts[c], scale, q_later[c], None, bands_c)
        got.append(lax.ppermute(pay, "tm", [(j, i) for i, j in sooner]))
        states.append(attend(first, counts[c], scale, q, flags_own, bands_c))
    out = final_call(counts, scale, q, states, got, pieces)
    return out.reshape(queries.shape)


def solution(mesh):
    spec = P("tm", "height", None, None)
    return jax.shard_map(
        shards,
        mesh=mesh,
        in_specs=(spec, spec, spec, spec, P()),
        out_specs=spec,
        check_vma=False,
    )
```
